32 devices in a mesh: wide: 8 (over z, x), narrow: 4 (over y, core).
Axes of the slice: x: 2, y: 2, z: 4, core: 2. Of those that a mesh axis runs over, the one named last changes fastest.
Arguments:
- tokens: bfloat16 [384, 2560], P(('wide', 'narrow')), may hold values from -6 to 6
- scores: float32 [384], P(('wide', 'narrow')), may hold values from 0.25 to 1
- expert_ids: int32 [384], P(('wide', 'narrow')), may hold values from 0 to 15, as said below
- gate_halves: bfloat16 [32, 2560, 2048], P(('wide', 'narrow')), may hold values from -0.125 to 0.125
- up_halves: bfloat16 [32, 2560, 2048], P(('wide', 'narrow')), may hold values from -0.125 to 0.125
- shared_gate: bfloat16 [2560, 4096], P(None, 'narrow'), may hold values from -0.125 to 0.125
- shared_up: bfloat16 [2560, 4096], P(None, 'narrow'), may hold values from -0.125 to 0.125
Outputs:
- routed_hidden: bfloat16 [384, 4096], P(('wide', 'narrow'))
- shared_hidden: bfloat16 [384, 4096], P('wide', 'narrow')
The draws below stay inside these ranges and needn't reach their ends.
Inputs may be any that keep to these rules, and one draw needn't show every extreme that they name: `expert_ids`: within the 12 rows of each device no expert is named more than 2 times, and one expert, the same for every device, is named exactly 2 times in the rows of every device.
All inputs are finite; a program needn't handle non-finite values.
Results may differ from the reference program's by a relative error of at most 0.0058.
Values may be sent and summed in bfloat16 or wider, within the bound.
A program may use at most 128 MiB of HBM per device.

```python
import jax
import jax.numpy as jnp
from jax import lax

D = 2560
FE = 4096
FS = 4096
CAP = 2
EXPERTS = 16
ROWS_DEV = 12
TOKENS = 384
DEVICES = 32


def draw_expert_ids(key, part):
    hot_key, rest_key = jax.random.split(jax.random.fold_in(key, 11))
    hot_expert = jax.random.randint(hot_key, (), 0, EXPERTS).astype(jnp.int32)
    block_keys = jax.random.split(rest_key, TOKENS // ROWS_DEV)

    def one_block(block_key):
        pick_key, place_key = jax.random.split(block_key)
        shuffled = jax.random.permutation(pick_key, (EXPERTS - 1) * CAP)
        others = (shuffled[:ROWS_DEV - CAP] // CAP).astype(jnp.int32)
        others = others + (others >= hot_expert).astype(jnp.int32)
        chosen = jnp.concatenate([jnp.full((CAP,), hot_expert, jnp.int32), others])
        return jax.random.permutation(place_key, chosen)
    return jax.vmap(one_block)(block_keys).reshape(TOKENS).astype(jnp.int32)


def level_of(own_key, extent, shards, least, largest):
    gain = 1.0
    for axis_at, shards_of in shards:
        steps = jax.random.uniform(jax.random.fold_in(jax.random.fold_in(own_key, 6), axis_at), (shards_of,), jnp.float32, least / len(shards), largest / len(shards))
        gain = gain * jnp.repeat(jnp.exp(steps), extent[axis_at] // shards_of).reshape((-1,) + (1,) * (len(extent) - 1 - axis_at))
    return gain


def scatter_about(own_key, dims, width, bound, cuts=(), kind=jnp.bfloat16):
    result = jax.random.normal(own_key, dims, jnp.float32) * width
    if len(cuts) > 0:
        result = level_of(own_key, dims, cuts, -0.22, 0.18) * result
    return jnp.clip(result, min=-bound, max=bound).astype(kind)


def setup_inputs(seed: int = 0) -> dict:
    streams_of = jax.random.split(jax.random.key(seed), 8)
    tokens = scatter_about(streams_of[0], (TOKENS, D), 1.0, 6.0, ((0, 32),))
    scores = jnp.clip(0.25 + 0.75 * jax.random.uniform(streams_of[1], (TOKENS,), jnp.float32) ** level_of(streams_of[1], (TOKENS,), ((0, 32),), -0.2, 0.2), 0.25, 1.0)
    expert_ids = draw_expert_ids(jax.random.fold_in(streams_of[7], 71), 0)
    gate_halves = scatter_about(streams_of[3], (2 * EXPERTS, D, FE // 2), D ** -0.5, 0.125, ((0, 32),))
    up_halves = scatter_about(streams_of[4], (2 * EXPERTS, D, FE // 2), D ** -0.5, 0.125, ((0, 32),))
    shared_gate = scatter_about(streams_of[5], (D, FS), D ** -0.5, 0.125, ((1, 4),))
    shared_up = scatter_about(streams_of[6], (D, FS), D ** -0.5, 0.125, ((1, 4),))
    return {"tokens": tokens, "scores": scores, "expert_ids": expert_ids, "gate_halves": gate_halves, "up_halves": up_halves, "shared_gate": shared_gate, "shared_up": shared_up}


def swiglu_rows(inputs, gate_matrix, up_matrix):
    gate_val = jnp.dot(inputs, gate_matrix, preferred_element_type=jnp.float32)
    up_val = jnp.dot(inputs, up_matrix, preferred_element_type=jnp.float32)
    return (jax.nn.silu(gate_val) * up_val).astype(jnp.bfloat16)


def reference(tokens, scores, expert_ids, gate_halves, up_halves, shared_gate, shared_up):
    scaled = (tokens.astype(jnp.float32) * scores[:, None]).astype(jnp.bfloat16)
    capacity = CAP * DEVICES

    def one_expert(expert):
        members = jnp.nonzero(expert_ids == expert, size=capacity, fill_value=TOKENS)[0]
        picked = jnp.take(scaled, members, axis=0, mode="clip")
        gate_full = jnp.concatenate([gate_halves[2 * expert], gate_halves[2 * expert + 1]], axis=1)
        up_full = jnp.concatenate([up_halves[2 * expert], up_halves[2 * expert + 1]], axis=1)
        return swiglu_rows(picked, gate_full, up_full), members

    hidden, members = lax.map(one_expert, jnp.arange(EXPERTS, dtype=jnp.int32))
    routed = jnp.zeros((TOKENS, FE), jnp.bfloat16)
    routed = routed.at[members.reshape(-1)].set(hidden.reshape(-1, FE), mode="drop")
    shared = swiglu_rows(tokens, shared_gate, shared_up)
    return routed, shared
```

```python
import functools

import jax
import jax.numpy as jnp
from jax import lax
from jax.experimental import pallas as pl
from jax.experimental.pallas import tpu as pltpu
from jax.sharding import PartitionSpec as P

CAP = 2
FULL = 128
PARTS = 1
CHUNKS = 2
TILE = 512
MESH = pl.DeviceIdType.MESH


def silu_mul(gate_val, up_val):
    return (gate_val / (1.0 + jnp.exp(-gate_val))) * up_val


def tiles(total, most):
    size = min(most, total)
    return [pl.ds(first, size) for first in range(0, total, size)]


def kernel(
    wide, narrow,
    tokens_hbm, scores_hbm, ids_hbm, gate_ref, up_ref, sgate_ref, sup_ref,
    routed_ref, shared_ref,
    tokens_ref, scores_ref, ids_ref,
    wg, wu, sg, su, tok_all, outgoing, incoming, rows_x, gate_sum, up_sum, sending, returned, flat,
    in_sem, weight_sem, tok_send, tok_recv, out_send, out_recv, pair_send, pair_recv, back_send, back_recv,
):
    devices = wide * narrow
    chips = devices // 2
    my_w = lax.axis_index("wide")
    my_n = lax.axis_index("narrow")
    me = my_w * narrow + my_n
    my_chip = me // 2
    my_core = me % 2
    rows, width = tokens_ref.shape
    padded = -(-rows // 16) * 16
    half_units = gate_ref.shape[2]
    experts = chips
    cells = experts * CAP
    slots = devices * CAP
    depth = width // PARTS
    part = half_units // CHUNKS
    shared_units = sgate_ref.shape[1]

    def dev(p):
        return (lax.div(p, narrow), lax.rem(p, narrow))

    partner = dev(my_chip * 2 + 1 - my_core)

    barrier = pltpu.get_barrier_semaphore()
    for k in range(1, devices):
        pl.semaphore_signal(barrier, inc=1, device_id=dev(lax.rem(me + k, devices)), device_id_type=MESH)

    small = [
        pltpu.make_async_copy(tokens_hbm, tokens_ref, in_sem.at[0]),
        pltpu.make_async_copy(scores_hbm, scores_ref, in_sem.at[1]),
        pltpu.make_async_copy(ids_hbm, ids_ref, in_sem.at[2]),
    ]
    for copy in small:
        copy.start()
    for ref, used in ((rows_x, slots), (tok_all, narrow * padded)):
        if ref.shape[0] > used:
            ref[used:, :] = jnp.zeros((ref.shape[0] - used, width), jnp.bfloat16)
    for copy in small:
        copy.wait()

    weight_copies = []
    for p in range(PARTS):
        deep = pl.ds(p * depth, depth)
        weight_copies.append(pltpu.make_async_copy(gate_ref.at[0, deep, :], wg.at[deep, :], weight_sem.at[2 * p]))
        weight_copies.append(pltpu.make_async_copy(up_ref.at[0, deep, :], wu.at[deep, :], weight_sem.at[2 * p + 1]))
    weight_copies.append(pltpu.make_async_copy(sgate_ref, sg, weight_sem.at[2 * PARTS]))
    weight_copies.append(pltpu.make_async_copy(sup_ref, su, weight_sem.at[2 * PARTS + 1]))
    for copy in weight_copies:
        copy.start()

    tok = tokens_ref[...]
    r_sub = lax.broadcasted_iota(jnp.int32, (rows, rows), 0)
    r_lane = lax.broadcasted_iota(jnp.int32, (rows, rows), 1)
    eye = r_sub == r_lane
    scores_col = jnp.sum(jnp.where(eye, scores_ref[...], 0.0), axis=1, keepdims=True)
    idsf_lane = ids_ref[...].astype(jnp.float32)
    ids_col = jnp.sum(jnp.where(eye, idsf_lane, 0.0), axis=1, keepdims=True)
    same = ids_col == idsf_lane
    rank_lane = jnp.sum(jnp.where(same & (r_sub < r_lane), 1.0, 0.0), axis=0, keepdims=True)
    rank_col = jnp.sum(jnp.where(same & (r_lane < r_sub), 1.0, 0.0), axis=1, keepdims=True)
    slot_lane = (idsf_lane * CAP + rank_lane).astype(jnp.int32)
    slot_col = (ids_col * CAP + rank_col).astype(jnp.int32)
    place = jnp.where(
        lax.broadcasted_iota(jnp.int32, (cells, rows), 0) == slot_lane, 1.0, 0.0
    ).astype(jnp.bfloat16)
    pick = jnp.where(
        lax.broadcasted_iota(jnp.int32, (rows, cells), 1) == slot_col, 1.0, 0.0
    ).astype(jnp.bfloat16)
    scaled = (tok.astype(jnp.float32) * scores_col).astype(jnp.bfloat16)
    placed = jnp.dot(place, scaled, preferred_element_type=jnp.float32).astype(jnp.bfloat16)
    for p in range(PARTS):
        for e in range(experts):
            outgoing[p, e] = placed[CAP * e : CAP * e + CAP, p * depth : p * depth + depth]
    my_tok = pl.ds(pl.multiple_of(my_n * padded, padded), padded)
    if padded > rows:
        tok_all[my_tok, :] = jnp.concatenate(
            [tok, jnp.zeros((padded - rows, width), jnp.bfloat16)], axis=0
        )
    else:
        tok_all[my_tok, :] = tok

    pl.semaphore_wait(barrier, devices - 1)

    lanes = narrow // 2
    my_lane = my_n // 2
    pair_n = my_lane * 2 + 1 - my_core

    for p in range(PARTS):
        for k in range(1, chips):
            chip = lax.rem(my_chip + k, chips)
            pltpu.make_async_remote_copy(
                src_ref=outgoing.at[p, chip], dst_ref=incoming.at[p, my_core, my_chip],
                send_sem=out_send.at[p], recv_sem=out_recv.at[p],
                device_id=dev(chip * 2 + my_core), device_id_type=MESH,
            ).start()

    def tok_slab(n):
        return tok_all.at[pl.ds(pl.multiple_of(n * padded, padded), padded), :]

    def tok_copy(k, n):
        to = ((my_lane + k) % lanes) * 2 + my_core
        return pltpu.make_async_remote_copy(
            src_ref=tok_slab(n), dst_ref=tok_slab(n),
            send_sem=tok_send.at[k], recv_sem=tok_recv.at[k],
            device_id=(my_w, to), device_id_type=MESH,
        )

    def tok_pass(k, n):
        return pltpu.make_async_remote_copy(
            src_ref=tok_slab(n), dst_ref=tok_slab(n),
            send_sem=tok_send.at[lanes + k], recv_sem=tok_recv.at[lanes + k],
            device_id=(my_w, pair_n), device_id_type=MESH,
        )

    for k in range(1, lanes):
        tok_copy(k, my_n).start()
    tok_pass(0, my_n).start()
    for p in range(PARTS):
        incoming[p, my_core, my_chip] = outgoing[p, my_chip]

    others = pl.ds(0, chips - 1)

    def all_out(p):
        return pltpu.make_async_remote_copy(
            src_ref=outgoing.at[p, others], dst_ref=incoming.at[p, my_core, others],
            send_sem=out_send.at[p], recv_sem=out_recv.at[p],
            device_id=partner, device_id_type=MESH,
        )

    def pair_copy(p, core):
        return pltpu.make_async_remote_copy(
            src_ref=incoming.at[p, core], dst_ref=incoming.at[p, core],
            send_sem=pair_send.at[p], recv_sem=pair_recv.at[p],
            device_id=partner, device_id_type=MESH,
        )

    def fill_rows(p, core):
        first = pl.multiple_of(core * cells, cells)
        half = rows_x.at[pl.ds(first, cells), pl.ds(p * depth, depth)]
        for s in range(chips):
            half[CAP * s : CAP * s + CAP, :] = incoming[p, core, s]

    def gather_rows(p):
        all_out(p).wait_recv()
        pair_copy(p, my_core).start()
        fill_rows(p, my_core)
        pair_copy(p, 1 - my_core).wait_recv()
        fill_rows(p, 1 - my_core)

    my_slot = my_core * chips + my_chip

    def back_copy(j, p):
        return pltpu.make_async_remote_copy(
            src_ref=sending.at[j, (p % 2) * chips + p // 2],
            dst_ref=returned.at[j, my_slot],
            send_sem=back_send.at[j], recv_sem=back_recv.at[j],
            device_id=dev(p), device_id_type=MESH,
        )

    def all_back(j):
        rest = pl.ds(0, devices - 1)
        return pltpu.make_async_remote_copy(
            src_ref=sending.at[j, rest], dst_ref=returned.at[j, rest],
            send_sem=back_send.at[j], recv_sem=back_recv.at[j],
            device_id=partner, device_id_type=MESH,
        )

    for p in range(PARTS):
        deep = pl.ds(p * depth, depth)
        gather_rows(p)
        if p == 0:
            for k in range(1, lanes):
                origin = ((my_lane + lanes - k) % lanes) * 2 + my_core
                tok_copy(k, origin).wait_recv()
                tok_pass(k, origin).start()
        weight_copies[2 * p].wait()
        weight_copies[2 * p + 1].wait()
        for j in range(CHUNKS):
            for local in tiles(part, TILE):
                cols = pl.ds(j * part + local.start, local.size)
                gate_val = jnp.dot(rows_x[:, deep], wg[deep, cols], preferred_element_type=jnp.float32)[:slots]
                up_val = jnp.dot(rows_x[:, deep], wu[deep, cols], preferred_element_type=jnp.float32)[:slots]
                if p > 0:
                    gate_val = gate_sum[:, cols] + gate_val
                    up_val = up_sum[:, cols] + up_val
                if p < PARTS - 1:
                    gate_sum[:, cols] = gate_val
                    up_sum[:, cols] = up_val
                    continue
                hidden = silu_mul(gate_val, up_val).astype(jnp.bfloat16)
                for s in range(devices):
                    sending[j, s, :, local] = hidden[CAP * s : CAP * s + CAP, :]
            if p == PARTS - 1:
                returned[j, my_slot] = sending[j, my_slot]
                for k in range(1, devices):
                    back_copy(j, lax.rem(me + k, devices)).start()

    for k in range(lanes):
        origin = ((my_lane + lanes - k) % lanes) * 2 + 1 - my_core
        tok_pass(k, origin).wait_recv()
    weight_copies[2 * PARTS].wait()
    weight_copies[2 * PARTS + 1].wait()
    for cols in tiles(shared_units, TILE):
        gate_val = jnp.dot(tok_all[...], sg[:, cols], preferred_element_type=jnp.float32)
        up_val = jnp.dot(tok_all[...], su[:, cols], preferred_element_type=jnp.float32)
        for n in range(narrow):
            some = slice(n * padded, n * padded + rows)
            shared_ref[n * rows : n * rows + rows, cols] = silu_mul(gate_val[some], up_val[some]).astype(jnp.bfloat16)

    for j in range(CHUNKS):
        all_back(j).wait_recv()
        for h in range(2):
            for e in range(experts):
                flat[CAP * e : CAP * e + CAP, :] = returned[j, h * experts + e]
            got = jnp.dot(pick, flat[...], preferred_element_type=jnp.float32)
            start = h * half_units + j * part
            routed_ref[:, start : start + part] = got.astype(jnp.bfloat16)

    for k in range(1, lanes):
        tok_copy(k, my_n).wait_send()
    for k in range(lanes):
        tok_pass(k, my_n).wait_send()
    for p in range(PARTS):
        pair_copy(p, my_core).wait_send()
        all_out(p).wait_send()
    for j in range(CHUNKS):
        all_back(j).wait_send()


def hand_on(routed_in, shared_in, routed_out, shared_out):
    routed_out[...] = routed_in[...]
    shared_out[...] = shared_in[...]


def shards(wide, narrow, tokens, scores, expert_ids, gate_halves, up_halves, shared_gate, shared_up):
    devices = wide * narrow
    chips = devices // 2
    rows, width = tokens.shape
    half_units = gate_halves.shape[2]
    shared_units = shared_gate.shape[1]
    padded = -(-rows // 16) * 16
    slots = devices * CAP
    part = half_units // CHUNKS
    depth = width // PARTS
    bf16 = jnp.bfloat16
    vmem = pl.BlockSpec(memory_space=pltpu.VMEM)
    hbm = pl.BlockSpec(memory_space=pl.ANY)
    dma = pltpu.SemaphoreType.DMA
    routed_shape = (rows, 2 * half_units)
    shared_shape = (rows * narrow, shared_units)
    outs = pl.pallas_call(
        functools.partial(kernel, wide, narrow),
        out_shape=(pltpu.VMEM(routed_shape, bf16), pltpu.VMEM(shared_shape, bf16)),
        in_specs=[hbm] * 7,
        out_specs=(vmem, vmem),
        scratch_shapes=[
            pltpu.VMEM((rows, width), bf16),
            pltpu.VMEM((1, rows), jnp.float32),
            pltpu.VMEM((1, rows), jnp.int32),
            pltpu.VMEM((width, half_units), bf16),
            pltpu.VMEM((width, half_units), bf16),
            pltpu.VMEM((width, shared_units), bf16),
            pltpu.VMEM((width, shared_units), bf16),
            pltpu.VMEM((max(narrow * padded, FULL), width), bf16),
            pltpu.VMEM((PARTS, chips, CAP, depth), bf16),
            pltpu.VMEM((PARTS, 2, chips, CAP, depth), bf16),
            pltpu.VMEM((max(slots, FULL), width), bf16),
            pltpu.VMEM((slots, half_units), jnp.float32),
            pltpu.VMEM((slots, half_units), jnp.float32),
            pltpu.VMEM((CHUNKS, devices, CAP, part), bf16),
            pltpu.VMEM((CHUNKS, devices, CAP, part), bf16),
            pltpu.VMEM((chips * CAP, part), bf16),
            dma((3,)),
            dma((2 * PARTS + 2,)),
            dma((narrow,)),
            dma((narrow,)),
            dma((PARTS,)),
            dma((PARTS,)),
            dma((PARTS,)),
            dma((PARTS,)),
            dma((CHUNKS,)),
            dma((CHUNKS,)),
        ],
        compiler_params=pltpu.CompilerParams(collective_id=0, has_side_effects=True, vmem_limit_bytes=60 * 1024 * 1024),
    )(tokens, scores[None, :], expert_ids[None, :], gate_halves, up_halves, shared_gate, shared_up)
    outs = [pltpu.with_memory_space_constraint(o, pltpu.VMEM) for o in outs]
    return pl.pallas_call(
        hand_on,
        out_shape=(jax.ShapeDtypeStruct(routed_shape, bf16), jax.ShapeDtypeStruct(shared_shape, bf16)),
        in_specs=[vmem, vmem],
        out_specs=(vmem, vmem),
    )(*outs)


def solution(mesh):
    placed = (
        P(("wide", "narrow"), None),
        P(("wide", "narrow")),
        P(("wide", "narrow")),
        P(("wide", "narrow"), None, None),
        P(("wide", "narrow"), None, None),
        P(None, "narrow"),
        P(None, "narrow"),
    )
    return jax.shard_map(
        functools.partial(shards, mesh.shape["wide"], mesh.shape["narrow"]),
        mesh=mesh,
        in_specs=placed,
        out_specs=(P(("wide", "narrow"), None), P("wide", "narrow")),
        check_vma=False,
    )
```

```python
import functools

import jax
import jax.numpy as jnp
from jax import lax
from jax.experimental import pallas as pl
from jax.experimental.pallas import tpu as pltpu
from jax.sharding import PartitionSpec as P

CAP = 2
FULL = 128
PARTS = 1
CHUNKS = 2
TILE = 512
MESH = pl.DeviceIdType.MESH


def silu_mul(gate_val, up_val):
    return (gate_val / (1.0 + jnp.exp(-gate_val))) * up_val


def tiles(first, last, most):
    return [pl.ds(at, min(most, last - at)) for at in range(first, last, most)]


def kernel(
    wide, narrow,
    tokens_hbm, scores_hbm, ids_hbm, gate_ref, up_ref, sgate_ref, sup_ref,
    routed_ref, shared_ref,
    tokens_ref, scores_ref, ids_ref,
    wg, wu, sg, su, tok_all, outgoing, incoming, rows_x, gate_sum, up_sum, sending, returned, flat,
    in_sem, weight_sem, tok_send, tok_recv, out_send, out_recv, pair_send, pair_recv, back_send, back_recv,
):
    devices = wide * narrow
    chips = devices // 2
    my_w = lax.axis_index("wide")
    my_n = lax.axis_index("narrow")
    me = my_w * narrow + my_n
    my_chip = me // 2
    my_core = me % 2
    rows, width = tokens_ref.shape
    padded = -(-rows // 16) * 16
    half_units = gate_ref.shape[2]
    experts = chips
    cells = experts * CAP
    slots = devices * CAP
    depth = width // PARTS
    part = half_units // CHUNKS
    shared_units = sgate_ref.shape[1]

    def dev(p):
        return (lax.div(p, narrow), lax.rem(p, narrow))

    partner = dev(my_chip * 2 + 1 - my_core)

    barrier = pltpu.get_barrier_semaphore()
    for k in range(1, devices):
        pl.semaphore_signal(barrier, inc=1, device_id=dev(lax.rem(me + k, devices)), device_id_type=MESH)

    small = [
        pltpu.make_async_copy(tokens_hbm, tokens_ref, in_sem.at[0]),
        pltpu.make_async_copy(scores_hbm, scores_ref, in_sem.at[1]),
        pltpu.make_async_copy(ids_hbm, ids_ref, in_sem.at[2]),
    ]
    for copy in small:
        copy.start()
    for ref, used in ((rows_x, slots), (tok_all, narrow * padded)):
        if ref.shape[0] > used:
            ref[used:, :] = jnp.zeros((ref.shape[0] - used, width), jnp.bfloat16)
    for copy in small:
        copy.wait()

    weight_copies = []
    for p in range(PARTS):
        deep = pl.ds(p * depth, depth)
        weight_copies.append(pltpu.make_async_copy(gate_ref.at[0, deep, :], wg.at[deep, :], weight_sem.at[2 * p]))
        weight_copies.append(pltpu.make_async_copy(up_ref.at[0, deep, :], wu.at[deep, :], weight_sem.at[2 * p + 1]))
    weight_copies.append(pltpu.make_async_copy(sgate_ref, sg, weight_sem.at[2 * PARTS]))
    weight_copies.append(pltpu.make_async_copy(sup_ref, su, weight_sem.at[2 * PARTS + 1]))
    for copy in weight_copies:
        copy.start()

    tok = tokens_ref[...]
    r_sub = lax.broadcasted_iota(jnp.int32, (rows, rows), 0)
    r_lane = lax.broadcasted_iota(jnp.int32, (rows, rows), 1)
    eye = r_sub == r_lane
    scores_col = jnp.sum(jnp.where(eye, scores_ref[...], 0.0), axis=1, keepdims=True)
    idsf_lane = ids_ref[...].astype(jnp.float32)
    ids_col = jnp.sum(jnp.where(eye, idsf_lane, 0.0), axis=1, keepdims=True)
    same = ids_col == idsf_lane
    rank_lane = jnp.sum(jnp.where(same & (r_sub < r_lane), 1.0, 0.0), axis=0, keepdims=True)
    rank_col = jnp.sum(jnp.where(same & (r_lane < r_sub), 1.0, 0.0), axis=1, keepdims=True)
    slot_lane = (idsf_lane * CAP + rank_lane).astype(jnp.int32)
    slot_col = (ids_col * CAP + rank_col).astype(jnp.int32)
    place = jnp.where(
        lax.broadcasted_iota(jnp.int32, (cells, rows), 0) == slot_lane, 1.0, 0.0
    ).astype(jnp.bfloat16)
    pick = jnp.where(
        lax.broadcasted_iota(jnp.int32, (rows, cells), 1) == slot_col, 1.0, 0.0
    ).astype(jnp.bfloat16)
    scaled = (tok.astype(jnp.float32) * scores_col).astype(jnp.bfloat16)
    placed = jnp.dot(place, scaled, preferred_element_type=jnp.float32).astype(jnp.bfloat16)
    for p in range(PARTS):
        for e in range(experts):
            outgoing[p, e] = placed[CAP * e : CAP * e + CAP, p * depth : p * depth + depth]
    my_tok = pl.ds(pl.multiple_of(my_n * padded, padded), padded)
    if padded > rows:
        tok_all[my_tok, :] = jnp.concatenate(
            [tok, jnp.zeros((padded - rows, width), jnp.bfloat16)], axis=0
        )
    else:
        tok_all[my_tok, :] = tok

    pl.semaphore_wait(barrier, devices - 1)

    lanes = narrow // 2
    my_lane = my_n // 2
    pair_n = my_lane * 2 + 1 - my_core

    for p in range(PARTS):
        for k in [*range(1, chips, 2), *range(2, chips, 2)]:
            chip = lax.rem(my_chip + k, chips)
            pltpu.make_async_remote_copy(
                src_ref=outgoing.at[p, chip], dst_ref=incoming.at[p, my_core, my_chip],
                send_sem=out_send.at[p], recv_sem=out_recv.at[p],
                device_id=dev(chip * 2 + my_core), device_id_type=MESH,
            ).start()

    def tok_slab(n):
        return tok_all.at[pl.ds(pl.multiple_of(n * padded, padded), padded), :]

    def tok_copy(k, n):
        to = ((my_lane + k) % lanes) * 2 + my_core
        return pltpu.make_async_remote_copy(
            src_ref=tok_slab(n), dst_ref=tok_slab(n),
            send_sem=tok_send.at[k], recv_sem=tok_recv.at[k],
            device_id=(my_w, to), device_id_type=MESH,
        )

    def tok_pass(k, n):
        return pltpu.make_async_remote_copy(
            src_ref=tok_slab(n), dst_ref=tok_slab(n),
            send_sem=tok_send.at[lanes + k], recv_sem=tok_recv.at[lanes + k],
            device_id=(my_w, pair_n), device_id_type=MESH,
        )

    for k in range(1, lanes):
        tok_copy(k, my_n).start()
    tok_pass(0, my_n).start()
    for p in range(PARTS):
        incoming[p, my_core, my_chip] = outgoing[p, my_chip]

    others = pl.ds(0, chips - 1)

    def all_out(p):
        return pltpu.make_async_remote_copy(
            src_ref=outgoing.at[p, others], dst_ref=incoming.at[p, my_core, others],
            send_sem=out_send.at[p], recv_sem=out_recv.at[p],
            device_id=partner, device_id_type=MESH,
        )

    def pair_copy(p, core):
        return pltpu.make_async_remote_copy(
            src_ref=incoming.at[p, core], dst_ref=incoming.at[p, core],
            send_sem=pair_send.at[p], recv_sem=pair_recv.at[p],
            device_id=partner, device_id_type=MESH,
        )

    def fill_rows(p, core):
        first = pl.multiple_of(core * cells, cells)
        half = rows_x.at[pl.ds(first, cells), pl.ds(p * depth, depth)]
        for s in range(chips):
            half[CAP * s : CAP * s + CAP, :] = incoming[p, core, s]

    def gather_rows(p):
        all_out(p).wait_recv()
        pair_copy(p, my_core).start()
        fill_rows(p, my_core)
        pair_copy(p, 1 - my_core).wait_recv()
        fill_rows(p, 1 - my_core)

    my_slot = my_core * chips + my_chip

    def chunk(j):
        return pl.ds(pl.multiple_of(j * part, part), part)

    def back_copy(j, p):
        return pltpu.make_async_remote_copy(
            src_ref=sending.at[(p % 2) * chips + p // 2, :, chunk(j)],
            dst_ref=returned.at[my_slot, :, chunk(j)],
            send_sem=back_send.at[j], recv_sem=back_recv.at[j],
            device_id=dev(p), device_id_type=MESH,
        )

    def all_back(j):
        rest = pl.ds(0, devices - 1)
        return pltpu.make_async_remote_copy(
            src_ref=sending.at[rest, :, chunk(j)], dst_ref=returned.at[rest, :, chunk(j)],
            send_sem=back_send.at[j], recv_sem=back_recv.at[j],
            device_id=partner, device_id_type=MESH,
        )

    for p in range(PARTS):
        deep = pl.ds(p * depth, depth)
        gather_rows(p)
        weight_copies[2 * p].wait()
        weight_copies[2 * p + 1].wait()
        def routed_step(j, carry):
            for at in range(0, part, 512):
                cols = pl.ds(pl.multiple_of(j * part + at, 512), 512)
                gate_val = jnp.dot(rows_x[...], wg[:, cols], preferred_element_type=jnp.float32)[:slots]
                up_val = jnp.dot(rows_x[...], wu[:, cols], preferred_element_type=jnp.float32)[:slots]
                hidden = silu_mul(gate_val, up_val).astype(jnp.bfloat16)
                for s in range(devices):
                    sending[s, :, cols] = hidden[CAP * s : CAP * s + CAP, :]
            returned[my_slot, :, chunk(j)] = sending[my_slot, :, chunk(j)]
            for k in range(1, devices):
                back_copy(j, lax.rem(me + k, devices)).start()
            return carry

        lax.fori_loop(0, CHUNKS, routed_step, 0)
        for k in range(1, lanes):
            origin = ((my_lane + lanes - k) % lanes) * 2 + my_core
            tok_copy(k, origin).wait_recv()
            tok_pass(k, origin).start()

    for k in range(lanes):
        origin = ((my_lane + lanes - k) % lanes) * 2 + 1 - my_core
        tok_pass(k, origin).wait_recv()
    weight_copies[2 * PARTS].wait()
    weight_copies[2 * PARTS + 1].wait()
    for cols in tiles(0, shared_units, TILE):
        gate_val = jnp.dot(tok_all[...], sg[:, cols], preferred_element_type=jnp.float32)
        up_val = jnp.dot(tok_all[...], su[:, cols], preferred_element_type=jnp.float32)
        for n in range(narrow):
            some = slice(n * padded, n * padded + rows)
            shared_ref[n * rows : n * rows + rows, cols] = silu_mul(gate_val[some], up_val[some]).astype(jnp.bfloat16)

    for j in range(CHUNKS):
        all_back(j).wait_recv()
        for h in range(2):
            for e in range(experts):
                flat[CAP * e : CAP * e + CAP, chunk(j)] = returned[h * experts + e, :, chunk(j)]
            got = jnp.dot(pick, flat[:, chunk(j)], preferred_element_type=jnp.float32)
            start = h * half_units + j * part
            routed_ref[:, start : start + part] = got.astype(jnp.bfloat16)

    for k in range(1, lanes):
        tok_copy(k, my_n).wait_send()
    for k in range(lanes):
        tok_pass(k, my_n).wait_send()
    for p in range(PARTS):
        pair_copy(p, my_core).wait_send()
        all_out(p).wait_send()
    for j in range(CHUNKS):
        all_back(j).wait_send()


def hand_on(routed_in, shared_in, routed_out, shared_out):
    routed_out[...] = routed_in[...]
    shared_out[...] = shared_in[...]


def shards(wide, narrow, tokens, scores, expert_ids, gate_halves, up_halves, shared_gate, shared_up):
    devices = wide * narrow
    chips = devices // 2
    rows, width = tokens.shape
    half_units = gate_halves.shape[2]
    shared_units = shared_gate.shape[1]
    padded = -(-rows // 16) * 16
    slots = devices * CAP
    depth = width // PARTS
    bf16 = jnp.bfloat16
    vmem = pl.BlockSpec(memory_space=pltpu.VMEM)
    hbm = pl.BlockSpec(memory_space=pl.ANY)
    dma = pltpu.SemaphoreType.DMA
    routed_shape = (rows, 2 * half_units)
    shared_shape = (rows * narrow, shared_units)
    outs = pl.pallas_call(
        functools.partial(kernel, wide, narrow),
        out_shape=(pltpu.VMEM(routed_shape, bf16), pltpu.VMEM(shared_shape, bf16)),
        in_specs=[hbm] * 7,
        out_specs=(vmem, vmem),
        scratch_shapes=[
            pltpu.VMEM((rows, width), bf16),
            pltpu.VMEM((1, rows), jnp.float32),
            pltpu.VMEM((1, rows), jnp.int32),
            pltpu.VMEM((width, half_units), bf16),
            pltpu.VMEM((width, half_units), bf16),
            pltpu.VMEM((width, shared_units), bf16),
            pltpu.VMEM((width, shared_units), bf16),
            pltpu.VMEM((max(narrow * padded, FULL), width), bf16),
            pltpu.VMEM((PARTS, chips, CAP, depth), bf16),
            pltpu.VMEM((PARTS, 2, chips, CAP, depth), bf16),
            pltpu.VMEM((max(slots, FULL), width), bf16),
            pltpu.VMEM((slots, half_units), jnp.float32),
            pltpu.VMEM((slots, half_units), jnp.float32),
            pltpu.VMEM((devices, CAP, half_units), bf16),
            pltpu.VMEM((devices, CAP, half_units), bf16),
            pltpu.VMEM((chips * CAP, half_units), bf16),
            dma((3,)),
            dma((2 * PARTS + 2,)),
            dma((narrow,)),
            dma((narrow,)),
            dma((PARTS,)),
            dma((PARTS,)),
            dma((PARTS,)),
            dma((PARTS,)),
            dma((CHUNKS,)),
            dma((CHUNKS,)),
        ],
        compiler_params=pltpu.CompilerParams(collective_id=0, has_side_effects=True, vmem_limit_bytes=60 * 1024 * 1024),
    )(tokens, scores[None, :], expert_ids[None, :], gate_halves, up_halves, shared_gate, shared_up)
    outs = [pltpu.with_memory_space_constraint(o, pltpu.VMEM) for o in outs]
    return pl.pallas_call(
        hand_on,
        out_shape=(jax.ShapeDtypeStruct(routed_shape, bf16), jax.ShapeDtypeStruct(shared_shape, bf16)),
        in_specs=[vmem, vmem],
        out_specs=(vmem, vmem),
    )(*outs)


def solution(mesh):
    placed = (
        P(("wide", "narrow"), None),
        P(("wide", "narrow")),
        P(("wide", "narrow")),
        P(("wide", "narrow"), None, None),
        P(("wide", "narrow"), None, None),
        P(None, "narrow"),
        P(None, "narrow"),
    )
    return jax.shard_map(
        functools.partial(shards, mesh.shape["wide"], mesh.shape["narrow"]),
        mesh=mesh,
        in_specs=placed,
        out_specs=(P(("wide", "narrow"), None), P("wide", "narrow")),
        check_vma=False,
    )
```

```python
import functools

import jax
import jax.numpy as jnp
from jax import lax
from jax.experimental import pallas as pl
from jax.experimental.pallas import tpu as pltpu
from jax.sharding import PartitionSpec as P

CAP = 2
FULL = 128
PARTS = 1
CHUNKS = 2
TILE = 512
MESH = pl.DeviceIdType.MESH


def silu_mul(gate_val, up_val):
    return (gate_val / (1.0 + jnp.exp(-gate_val))) * up_val


def tiles(first, last, most):
    return [pl.ds(at, min(most, last - at)) for at in range(first, last, most)]


def kernel(
    wide, narrow,
    tokens_hbm, scores_hbm, ids_hbm, gate_ref, up_ref, sgate_ref, sup_ref,
    routed_ref, shared_ref,
    tokens_ref, scores_ref, ids_ref,
    wg, wu, sg, su, tok_all, outgoing, incoming, rows_x, gate_sum, up_sum, sending, returned, flat,
    in_sem, weight_sem, tok_send, tok_recv, out_send, out_recv, pair_send, pair_recv, back_send, back_recv,
):
    devices = wide * narrow
    chips = devices // 2
    my_w = lax.axis_index("wide")
    my_n = lax.axis_index("narrow")
    me = my_w * narrow + my_n
    my_chip = me // 2
    my_core = me % 2
    rows, width = tokens_ref.shape
    padded = -(-rows // 16) * 16
    half_units = gate_ref.shape[2]
    experts = chips
    cells = experts * CAP
    slots = devices * CAP
    depth = width // PARTS
    part = half_units // CHUNKS
    shared_units = sgate_ref.shape[1]

    def dev(p):
        return (lax.div(p, narrow), lax.rem(p, narrow))

    partner = dev(my_chip * 2 + 1 - my_core)

    small = [
        pltpu.make_async_copy(tokens_hbm, tokens_ref, in_sem.at[0]),
        pltpu.make_async_copy(scores_hbm, scores_ref, in_sem.at[1]),
        pltpu.make_async_copy(ids_hbm, ids_ref, in_sem.at[2]),
    ]
    for copy in small:
        copy.start()
    barrier = pltpu.get_barrier_semaphore()
    for k in range(1, devices):
        pl.semaphore_signal(barrier, inc=1, device_id=dev(lax.rem(me + k, devices)), device_id_type=MESH)

    for ref, used in ((rows_x, slots), (tok_all, narrow * padded)):
        if ref.shape[0] > used:
            ref[used:, :] = jnp.zeros((ref.shape[0] - used, width), jnp.bfloat16)
    for copy in small:
        copy.wait()

    weight_copies = []
    for p in range(PARTS):
        deep = pl.ds(p * depth, depth)
        weight_copies.append(pltpu.make_async_copy(gate_ref.at[0, deep, :], wg.at[deep, :], weight_sem.at[2 * p]))
        weight_copies.append(pltpu.make_async_copy(up_ref.at[0, deep, :], wu.at[deep, :], weight_sem.at[2 * p + 1]))
    weight_copies.append(pltpu.make_async_copy(sgate_ref, sg, weight_sem.at[2 * PARTS]))
    weight_copies.append(pltpu.make_async_copy(sup_ref, su, weight_sem.at[2 * PARTS + 1]))
    for copy in weight_copies:
        copy.start()

    tok = tokens_ref[...]
    r_sub = lax.broadcasted_iota(jnp.int32, (rows, rows), 0)
    r_lane = lax.broadcasted_iota(jnp.int32, (rows, rows), 1)
    eye = r_sub == r_lane
    scores_col = jnp.sum(jnp.where(eye, scores_ref[...], 0.0), axis=1, keepdims=True)
    idsf_lane = ids_ref[...].astype(jnp.float32)
    ids_col = jnp.sum(jnp.where(eye, idsf_lane, 0.0), axis=1, keepdims=True)
    same = ids_col == idsf_lane
    rank_lane = jnp.sum(jnp.where(same & (r_sub < r_lane), 1.0, 0.0), axis=0, keepdims=True)
    rank_col = jnp.sum(jnp.where(same & (r_lane < r_sub), 1.0, 0.0), axis=1, keepdims=True)
    slot_lane = (idsf_lane * CAP + rank_lane).astype(jnp.int32)
    slot_col = (ids_col * CAP + rank_col).astype(jnp.int32)
    place = jnp.where(
        lax.broadcasted_iota(jnp.int32, (cells, rows), 0) == slot_lane, 1.0, 0.0
    ).astype(jnp.bfloat16)
    pick = jnp.where(
        lax.broadcasted_iota(jnp.int32, (rows, cells), 1) == slot_col, 1.0, 0.0
    ).astype(jnp.bfloat16)
    scaled = (tok.astype(jnp.float32) * scores_col).astype(jnp.bfloat16)
    placed = jnp.dot(place, scaled, preferred_element_type=jnp.float32).astype(jnp.bfloat16)
    for p in range(PARTS):
        for e in range(experts):
            outgoing[p, e] = placed[CAP * e : CAP * e + CAP, p * depth : p * depth + depth]
    my_tok = pl.ds(pl.multiple_of(my_n * padded, padded), padded)
    if padded > rows:
        tok_all[my_tok, :] = jnp.concatenate(
            [tok, jnp.zeros((padded - rows, width), jnp.bfloat16)], axis=0
        )
    else:
        tok_all[my_tok, :] = tok

    pl.semaphore_wait(barrier, devices - 1)

    lanes = narrow // 2
    my_lane = my_n // 2
    pair_n = my_lane * 2 + 1 - my_core

    for p in range(PARTS):
        for k in [*range(1, chips, 2), *range(2, chips, 4), *range(4, chips, 4)]:
            chip = lax.rem(my_chip + k, chips)
            pltpu.make_async_remote_copy(
                src_ref=outgoing.at[p, chip], dst_ref=incoming.at[p, my_core, my_chip],
                send_sem=out_send.at[p], recv_sem=out_recv.at[p],
                device_id=dev(chip * 2 + my_core), device_id_type=MESH,
            ).start()

    def tok_slab(n):
        return tok_all.at[pl.ds(pl.multiple_of(n * padded, padded), padded), :]

    def tok_copy(k, n):
        to = ((my_lane + k) % lanes) * 2 + my_core
        return pltpu.make_async_remote_copy(
            src_ref=tok_slab(n), dst_ref=tok_slab(n),
            send_sem=tok_send.at[k], recv_sem=tok_recv.at[k],
            device_id=(my_w, to), device_id_type=MESH,
        )

    def tok_pass(k, n):
        return pltpu.make_async_remote_copy(
            src_ref=tok_slab(n), dst_ref=tok_slab(n),
            send_sem=tok_send.at[lanes + k], recv_sem=tok_recv.at[lanes + k],
            device_id=(my_w, pair_n), device_id_type=MESH,
        )

    for p in range(PARTS):
        incoming[p, my_core, my_chip] = outgoing[p, my_chip]

    others = pl.ds(0, chips - 1)

    def all_out(p):
        return pltpu.make_async_remote_copy(
            src_ref=outgoing.at[p, others], dst_ref=incoming.at[p, my_core, others],
            send_sem=out_send.at[p], recv_sem=out_recv.at[p],
            device_id=partner, device_id_type=MESH,
        )

    def pair_copy(p, core):
        return pltpu.make_async_remote_copy(
            src_ref=incoming.at[p, core], dst_ref=incoming.at[p, core],
            send_sem=pair_send.at[p], recv_sem=pair_recv.at[p],
            device_id=partner, device_id_type=MESH,
        )

    def fill_rows(p, core):
        first = pl.multiple_of(core * cells, cells)
        half = rows_x.at[pl.ds(first, cells), pl.ds(p * depth, depth)]
        for s in range(chips):
            half[CAP * s : CAP * s + CAP, :] = incoming[p, core, s]

    def gather_rows(p):
        all_out(p).wait_recv()
        pair_copy(p, my_core).start()
        fill_rows(p, my_core)
        pair_copy(p, 1 - my_core).wait_recv()
        fill_rows(p, 1 - my_core)

    my_slot = my_core * chips + my_chip

    def chunk(j):
        return pl.ds(pl.multiple_of(j * part, part), part)

    def back_copy(j, p):
        return pltpu.make_async_remote_copy(
            src_ref=sending.at[(p % 2) * chips + p // 2, :, chunk(j)],
            dst_ref=returned.at[my_slot, :, chunk(j)],
            send_sem=back_send.at[j], recv_sem=back_recv.at[j],
            device_id=dev(p), device_id_type=MESH,
        )

    def all_back(j):
        rest = pl.ds(0, devices - 1)
        return pltpu.make_async_remote_copy(
            src_ref=sending.at[rest, :, chunk(j)], dst_ref=returned.at[rest, :, chunk(j)],
            send_sem=back_send.at[j], recv_sem=back_recv.at[j],
            device_id=partner, device_id_type=MESH,
        )

    for p in range(PARTS):
        deep = pl.ds(p * depth, depth)
        all_out(p).wait_recv()
        pair_copy(p, my_core).start()
        for k in range(1, lanes):
            tok_copy(k, my_n).start()
        tok_pass(0, my_n).start()
        fill_rows(p, my_core)
        pair_copy(p, 1 - my_core).wait_recv()
        fill_rows(p, 1 - my_core)
        weight_copies[2 * p].wait()
        weight_copies[2 * p + 1].wait()
        def routed_step(j, carry):
            for at in range(0, part, 512):
                cols = pl.ds(pl.multiple_of(j * part + at, 512), 512)
                gate_val = jnp.dot(rows_x[...], wg[:, cols], preferred_element_type=jnp.float32)[:slots]
                up_val = jnp.dot(rows_x[...], wu[:, cols], preferred_element_type=jnp.float32)[:slots]
                hidden = silu_mul(gate_val, up_val).astype(jnp.bfloat16)
                for s in range(devices):
                    sending[s, :, cols] = hidden[CAP * s : CAP * s + CAP, :]
            returned[my_slot, :, chunk(j)] = sending[my_slot, :, chunk(j)]
            for k in range(1, devices):
                back_copy(j, lax.rem(me + k, devices)).start()
            return carry

        lax.fori_loop(0, CHUNKS, routed_step, 0)
        for k in range(1, lanes):
            origin = ((my_lane + lanes - k) % lanes) * 2 + my_core
            tok_copy(k, origin).wait_recv()
            tok_pass(k, origin).start()

    for k in range(lanes):
        origin = ((my_lane + lanes - k) % lanes) * 2 + 1 - my_core
        tok_pass(k, origin).wait_recv()
    weight_copies[2 * PARTS].wait()
    weight_copies[2 * PARTS + 1].wait()
    for cols in tiles(0, shared_units, TILE):
        gate_val = jnp.dot(tok_all[...], sg[:, cols], preferred_element_type=jnp.float32)
        up_val = jnp.dot(tok_all[...], su[:, cols], preferred_element_type=jnp.float32)
        for n in range(narrow):
            some = slice(n * padded, n * padded + rows)
            shared_ref[n * rows : n * rows + rows, cols] = silu_mul(gate_val[some], up_val[some]).astype(jnp.bfloat16)

    for j in range(CHUNKS):
        all_back(j).wait_recv()
        for h in range(2):
            for e in range(experts):
                flat[CAP * e : CAP * e + CAP, chunk(j)] = returned[h * experts + e, :, chunk(j)]
            got = jnp.dot(pick, flat[:, chunk(j)], preferred_element_type=jnp.float32)
            start = h * half_units + j * part
            routed_ref[:, start : start + part] = got.astype(jnp.bfloat16)

    for k in range(1, lanes):
        tok_copy(k, my_n).wait_send()
    for k in range(lanes):
        tok_pass(k, my_n).wait_send()
    for p in range(PARTS):
        pair_copy(p, my_core).wait_send()
        all_out(p).wait_send()
    for j in range(CHUNKS):
        all_back(j).wait_send()


def hand_on(routed_in, shared_in, routed_out, shared_out):
    routed_out[...] = routed_in[...]
    shared_out[...] = shared_in[...]


def shards(wide, narrow, tokens, scores, expert_ids, gate_halves, up_halves, shared_gate, shared_up):
    devices = wide * narrow
    chips = devices // 2
    rows, width = tokens.shape
    half_units = gate_halves.shape[2]
    shared_units = shared_gate.shape[1]
    padded = -(-rows // 16) * 16
    slots = devices * CAP
    depth = width // PARTS
    bf16 = jnp.bfloat16
    vmem = pl.BlockSpec(memory_space=pltpu.VMEM)
    hbm = pl.BlockSpec(memory_space=pl.ANY)
    dma = pltpu.SemaphoreType.DMA
    routed_shape = (rows, 2 * half_units)
    shared_shape = (rows * narrow, shared_units)
    outs = pl.pallas_call(
        functools.partial(kernel, wide, narrow),
        out_shape=(pltpu.VMEM(routed_shape, bf16), pltpu.VMEM(shared_shape, bf16)),
        in_specs=[hbm] * 7,
        out_specs=(vmem, vmem),
        scratch_shapes=[
            pltpu.VMEM((rows, width), bf16),
            pltpu.VMEM((1, rows), jnp.float32),
            pltpu.VMEM((1, rows), jnp.int32),
            pltpu.VMEM((width, half_units), bf16),
            pltpu.VMEM((width, half_units), bf16),
            pltpu.VMEM((width, shared_units), bf16),
            pltpu.VMEM((width, shared_units), bf16),
            pltpu.VMEM((max(narrow * padded, FULL), width), bf16),
            pltpu.VMEM((PARTS, chips, CAP, depth), bf16),
            pltpu.VMEM((PARTS, 2, chips, CAP, depth), bf16),
            pltpu.VMEM((max(slots, FULL), width), bf16),
            pltpu.VMEM((slots, half_units), jnp.float32),
            pltpu.VMEM((slots, half_units), jnp.float32),
            pltpu.VMEM((devices, CAP, half_units), bf16),
            pltpu.VMEM((devices, CAP, half_units), bf16),
            pltpu.VMEM((chips * CAP, half_units), bf16),
            dma((3,)),
            dma((2 * PARTS + 2,)),
            dma((narrow,)),
            dma((narrow,)),
            dma((PARTS,)),
            dma((PARTS,)),
            dma((PARTS,)),
            dma((PARTS,)),
            dma((CHUNKS,)),
            dma((CHUNKS,)),
        ],
        compiler_params=pltpu.CompilerParams(collective_id=0, has_side_effects=True, vmem_limit_bytes=60 * 1024 * 1024),
    )(tokens, scores[None, :], expert_ids[None, :], gate_halves, up_halves, shared_gate, shared_up)
    outs = [pltpu.with_memory_space_constraint(o, pltpu.VMEM) for o in outs]
    return pl.pallas_call(
        hand_on,
        out_shape=(jax.ShapeDtypeStruct(routed_shape, bf16), jax.ShapeDtypeStruct(shared_shape, bf16)),
        in_specs=[vmem, vmem],
        out_specs=(vmem, vmem),
    )(*outs)


def solution(mesh):
    placed = (
        P(("wide", "narrow"), None),
        P(("wide", "narrow")),
        P(("wide", "narrow")),
        P(("wide", "narrow"), None, None),
        P(("wide", "narrow"), None, None),
        P(None, "narrow"),
        P(None, "narrow"),
    )
    return jax.shard_map(
        functools.partial(shards, mesh.shape["wide"], mesh.shape["narrow"]),
        mesh=mesh,
        in_specs=placed,
        out_specs=(P(("wide", "narrow"), None), P("wide", "narrow")),
        check_vma=False,
    )
```

```python
import functools

import jax
import jax.numpy as jnp
from jax import lax
from jax.experimental import pallas as pl
from jax.experimental.pallas import tpu as pltpu
from jax.sharding import PartitionSpec as P

CAP = 2
FULL = 128
PARTS = 1
CHUNKS = 2
TILE = 512
MESH = pl.DeviceIdType.MESH


def silu_mul(gate_val, up_val):
    return (gate_val / (1.0 + jnp.exp(-gate_val))) * up_val


def tiles(first, last, most):
    return [pl.ds(at, min(most, last - at)) for at in range(first, last, most)]


def kernel(
    wide, narrow,
    tokens_hbm, scores_hbm, ids_hbm, gate_ref, up_ref, sgate_ref, sup_ref,
    routed_ref, shared_ref,
    tokens_ref, scores_ref, ids_ref,
    wg, wu, sg, su, tok_all, outgoing, incoming, rows_x, gate_sum, up_sum, sending, returned, flat,
    in_sem, weight_sem, tok_send, tok_recv, out_send, out_recv, pair_send, pair_recv, back_send, back_recv,
):
    devices = wide * narrow
    chips = devices // 2
    my_w = lax.axis_index("wide")
    my_n = lax.axis_index("narrow")
    me = my_w * narrow + my_n
    my_chip = me // 2
    my_core = me % 2
    rows, width = tokens_ref.shape
    padded = -(-rows // 16) * 16
    half_units = gate_ref.shape[2]
    experts = chips
    cells = experts * CAP
    slots = devices * CAP
    depth = width // PARTS
    part = half_units // CHUNKS
    shared_units = sgate_ref.shape[1]

    def dev(p):
        return (lax.div(p, narrow), lax.rem(p, narrow))

    partner = dev(my_chip * 2 + 1 - my_core)

    small = [
        pltpu.make_async_copy(tokens_hbm, tokens_ref, in_sem.at[0]),
        pltpu.make_async_copy(scores_hbm, scores_ref, in_sem.at[1]),
        pltpu.make_async_copy(ids_hbm, ids_ref, in_sem.at[2]),
    ]
    for copy in small:
        copy.start()
    barrier = pltpu.get_barrier_semaphore()
    for k in range(1, devices):
        pl.semaphore_signal(barrier, inc=1, device_id=dev(lax.rem(me + k, devices)), device_id_type=MESH)

    weight_copies = []
    def weight_pair(j):
        cols = pl.ds(pl.multiple_of(j * part, part), part)
        return [
            pltpu.make_async_copy(gate_ref.at[0, :, cols], wg.at[:, cols], weight_sem.at[2 + 2 * j]),
            pltpu.make_async_copy(up_ref.at[0, :, cols], wu.at[:, cols], weight_sem.at[3 + 2 * j]),
        ]

    for j in range(CHUNKS):
        weight_copies.extend(weight_pair(j))
    weight_copies.append(pltpu.make_async_copy(sgate_ref, sg, weight_sem.at[0]))
    weight_copies.append(pltpu.make_async_copy(sup_ref, su, weight_sem.at[1]))
    for copy in weight_copies:
        copy.start(priority=1)
    for ref, used in ((rows_x, slots), (tok_all, narrow * padded)):
        if ref.shape[0] > used:
            ref[used:, :] = jnp.zeros((ref.shape[0] - used, width), jnp.bfloat16)
    for copy in small:
        copy.wait()


    tok = tokens_ref[...]
    r_sub = lax.broadcasted_iota(jnp.int32, (rows, rows), 0)
    r_lane = lax.broadcasted_iota(jnp.int32, (rows, rows), 1)
    eye = r_sub == r_lane
    scores_col = jnp.sum(jnp.where(eye, scores_ref[...], 0.0), axis=1, keepdims=True)
    idsf_lane = ids_ref[...].astype(jnp.float32)
    ids_col = jnp.sum(jnp.where(eye, idsf_lane, 0.0), axis=1, keepdims=True)
    same = ids_col == idsf_lane
    rank_lane = jnp.sum(jnp.where(same & (r_sub < r_lane), 1.0, 0.0), axis=0, keepdims=True)
    rank_col = jnp.sum(jnp.where(same & (r_lane < r_sub), 1.0, 0.0), axis=1, keepdims=True)
    slot_lane = (idsf_lane * CAP + rank_lane).astype(jnp.int32)
    slot_col = (ids_col * CAP + rank_col).astype(jnp.int32)
    place = jnp.where(
        lax.broadcasted_iota(jnp.int32, (cells, rows), 0) == slot_lane, 1.0, 0.0
    ).astype(jnp.bfloat16)
    pick = jnp.where(
        lax.broadcasted_iota(jnp.int32, (rows, cells), 1) == slot_col, 1.0, 0.0
    ).astype(jnp.bfloat16)
    scaled = (tok.astype(jnp.float32) * scores_col).astype(jnp.bfloat16)
    placed = jnp.dot(place, scaled, preferred_element_type=jnp.float32).astype(jnp.bfloat16)
    for p in range(PARTS):
        for e in range(experts):
            outgoing[p, e] = placed[CAP * e : CAP * e + CAP, p * depth : p * depth + depth]
    my_tok = pl.ds(pl.multiple_of(my_n * padded, padded), padded)
    if padded > rows:
        tok_all[my_tok, :] = jnp.concatenate(
            [tok, jnp.zeros((padded - rows, width), jnp.bfloat16)], axis=0
        )
    else:
        tok_all[my_tok, :] = tok

    pl.semaphore_wait(barrier, devices - 1)

    lanes = narrow // 2
    my_lane = my_n // 2
    pair_n = my_lane * 2 + 1 - my_core

    for p in range(PARTS):
        for k in [*range(1, chips, 2), *range(2, chips, 4), *range(4, chips, 4)]:
            chip = lax.rem(my_chip + k, chips)
            pltpu.make_async_remote_copy(
                src_ref=outgoing.at[p, chip], dst_ref=incoming.at[p, my_core, my_chip],
                send_sem=out_send.at[p], recv_sem=out_recv.at[p],
                device_id=dev(chip * 2 + my_core), device_id_type=MESH,
            ).start()

    def tok_slab(n):
        return tok_all.at[pl.ds(pl.multiple_of(n * padded, padded), padded), :]

    def tok_copy(k, n):
        to = ((my_lane + k) % lanes) * 2 + my_core
        return pltpu.make_async_remote_copy(
            src_ref=tok_slab(n), dst_ref=tok_slab(n),
            send_sem=tok_send.at[k], recv_sem=tok_recv.at[k],
            device_id=(my_w, to), device_id_type=MESH,
        )

    def tok_pass(k, n):
        return pltpu.make_async_remote_copy(
            src_ref=tok_slab(n), dst_ref=tok_slab(n),
            send_sem=tok_send.at[lanes + k], recv_sem=tok_recv.at[lanes + k],
            device_id=(my_w, pair_n), device_id_type=MESH,
        )

    for p in range(PARTS):
        incoming[p, my_core, my_chip] = outgoing[p, my_chip]

    others = pl.ds(0, chips - 1)

    def all_out(p):
        return pltpu.make_async_remote_copy(
            src_ref=outgoing.at[p, others], dst_ref=incoming.at[p, my_core, others],
            send_sem=out_send.at[p], recv_sem=out_recv.at[p],
            device_id=partner, device_id_type=MESH,
        )

    def pair_copy(p, core):
        return pltpu.make_async_remote_copy(
            src_ref=incoming.at[p, core], dst_ref=incoming.at[p, core],
            send_sem=pair_send.at[p], recv_sem=pair_recv.at[p],
            device_id=partner, device_id_type=MESH,
        )

    def fill_rows(p, core):
        first = pl.multiple_of(core * cells, cells)
        half = rows_x.at[pl.ds(first, cells), pl.ds(p * depth, depth)]
        for s in range(chips):
            half[CAP * s : CAP * s + CAP, :] = incoming[p, core, s]

    def gather_rows(p):
        all_out(p).wait_recv()
        pair_copy(p, my_core).start()
        fill_rows(p, my_core)
        pair_copy(p, 1 - my_core).wait_recv()
        fill_rows(p, 1 - my_core)

    my_slot = my_core * chips + my_chip

    def chunk(j):
        return pl.ds(pl.multiple_of(j * part, part), part)

    def back_copy(j, p):
        return pltpu.make_async_remote_copy(
            src_ref=sending.at[(p % 2) * chips + p // 2, :, chunk(j)],
            dst_ref=returned.at[my_slot, :, chunk(j)],
            send_sem=back_send.at[j], recv_sem=back_recv.at[j],
            device_id=dev(p), device_id_type=MESH,
        )

    def all_back(j):
        rest = pl.ds(0, devices - 1)
        return pltpu.make_async_remote_copy(
            src_ref=sending.at[rest, :, chunk(j)], dst_ref=returned.at[rest, :, chunk(j)],
            send_sem=back_send.at[j], recv_sem=back_recv.at[j],
            device_id=partner, device_id_type=MESH,
        )

    for p in range(PARTS):
        deep = pl.ds(p * depth, depth)
        all_out(p).wait_recv()
        pair_copy(p, my_core).start()
        for k in range(1, lanes):
            tok_copy(k, my_n).start()
        tok_pass(0, my_n).start()
        fill_rows(p, my_core)
        pair_copy(p, 1 - my_core).wait_recv()
        fill_rows(p, 1 - my_core)
        def routed_step(j, carry):
            for copy in weight_pair(j):
                copy.wait()
            for at in range(0, part, 512):
                cols = pl.ds(pl.multiple_of(j * part + at, 512), 512)
                gate_val = jnp.dot(rows_x[...], wg[:, cols], preferred_element_type=jnp.float32)[:slots]
                up_val = jnp.dot(rows_x[...], wu[:, cols], preferred_element_type=jnp.float32)[:slots]
                hidden = silu_mul(gate_val, up_val).astype(jnp.bfloat16)
                for s in range(devices):
                    sending[s, :, cols] = hidden[CAP * s : CAP * s + CAP, :]
            returned[my_slot, :, chunk(j)] = sending[my_slot, :, chunk(j)]
            for p0 in range(2):
                @pl.when(me != p0)
                def _():
                    back_copy(j, p0).start()
            for k in range(1, devices):
                @pl.when(lax.rem(me + k, devices) >= 2)
                def _():
                    back_copy(j, lax.rem(me + k, devices)).start()
            return carry

        lax.fori_loop(0, CHUNKS, routed_step, 0)
        for k in range(1, lanes):
            origin = ((my_lane + lanes - k) % lanes) * 2 + my_core
            tok_copy(k, origin).wait_recv()
            tok_pass(k, origin).start()

    for k in range(lanes):
        origin = ((my_lane + lanes - k) % lanes) * 2 + 1 - my_core
        tok_pass(k, origin).wait_recv()
    weight_copies[2 * CHUNKS].wait()
    weight_copies[2 * CHUNKS + 1].wait()
    for cols in tiles(0, shared_units, TILE):
        gate_val = jnp.dot(tok_all[...], sg[:, cols], preferred_element_type=jnp.float32)
        up_val = jnp.dot(tok_all[...], su[:, cols], preferred_element_type=jnp.float32)
        for n in range(narrow):
            some = slice(n * padded, n * padded + rows)
            shared_ref[n * rows : n * rows + rows, cols] = silu_mul(gate_val[some], up_val[some]).astype(jnp.bfloat16)

    for j in range(CHUNKS):
        all_back(j).wait_recv()
        for h in range(2):
            for e in range(experts):
                flat[CAP * e : CAP * e + CAP, chunk(j)] = returned[h * experts + e, :, chunk(j)]
            got = jnp.dot(pick, flat[:, chunk(j)], preferred_element_type=jnp.float32)
            start = h * half_units + j * part
            routed_ref[:, start : start + part] = got.astype(jnp.bfloat16)

    for k in range(1, lanes):
        tok_copy(k, my_n).wait_send()
    for k in range(lanes):
        tok_pass(k, my_n).wait_send()
    for p in range(PARTS):
        pair_copy(p, my_core).wait_send()
        all_out(p).wait_send()
    for j in range(CHUNKS):
        all_back(j).wait_send()


def hand_on(routed_in, shared_in, routed_out, shared_out):
    routed_out[...] = routed_in[...]
    shared_out[...] = shared_in[...]


def shards(wide, narrow, tokens, scores, expert_ids, gate_halves, up_halves, shared_gate, shared_up):
    devices = wide * narrow
    chips = devices // 2
    rows, width = tokens.shape
    half_units = gate_halves.shape[2]
    shared_units = shared_gate.shape[1]
    padded = -(-rows // 16) * 16
    slots = devices * CAP
    depth = width // PARTS
    bf16 = jnp.bfloat16
    vmem = pl.BlockSpec(memory_space=pltpu.VMEM)
    hbm = pl.BlockSpec(memory_space=pl.ANY)
    dma = pltpu.SemaphoreType.DMA
    routed_shape = (rows, 2 * half_units)
    shared_shape = (rows * narrow, shared_units)
    outs = pl.pallas_call(
        functools.partial(kernel, wide, narrow),
        out_shape=(pltpu.VMEM(routed_shape, bf16), pltpu.VMEM(shared_shape, bf16)),
        in_specs=[hbm] * 7,
        out_specs=(vmem, vmem),
        scratch_shapes=[
            pltpu.VMEM((rows, width), bf16),
            pltpu.VMEM((1, rows), jnp.float32),
            pltpu.VMEM((1, rows), jnp.int32),
            pltpu.VMEM((width, half_units), bf16),
            pltpu.VMEM((width, half_units), bf16),
            pltpu.VMEM((width, shared_units), bf16),
            pltpu.VMEM((width, shared_units), bf16),
            pltpu.VMEM((max(narrow * padded, FULL), width), bf16),
            pltpu.VMEM((PARTS, chips, CAP, depth), bf16),
            pltpu.VMEM((PARTS, 2, chips, CAP, depth), bf16),
            pltpu.VMEM((max(slots, FULL), width), bf16),
            pltpu.VMEM((slots, half_units), jnp.float32),
            pltpu.VMEM((slots, half_units), jnp.float32),
            pltpu.VMEM((devices, CAP, half_units), bf16),
            pltpu.VMEM((devices, CAP, half_units), bf16),
            pltpu.VMEM((chips * CAP, half_units), bf16),
            dma((3,)),
            dma((2 * CHUNKS + 2,)),
            dma((narrow,)),
            dma((narrow,)),
            dma((PARTS,)),
            dma((PARTS,)),
            dma((PARTS,)),
            dma((PARTS,)),
            dma((CHUNKS,)),
            dma((CHUNKS,)),
        ],
        compiler_params=pltpu.CompilerParams(collective_id=0, has_side_effects=True, vmem_limit_bytes=60 * 1024 * 1024),
    )(tokens, scores[None, :], expert_ids[None, :], gate_halves, up_halves, shared_gate, shared_up)
    outs = [pltpu.with_memory_space_constraint(o, pltpu.VMEM) for o in outs]
    return pl.pallas_call(
        hand_on,
        out_shape=(jax.ShapeDtypeStruct(routed_shape, bf16), jax.ShapeDtypeStruct(shared_shape, bf16)),
        in_specs=[vmem, vmem],
        out_specs=(vmem, vmem),
    )(*outs)


def solution(mesh):
    placed = (
        P(("wide", "narrow"), None),
        P(("wide", "narrow")),
        P(("wide", "narrow")),
        P(("wide", "narrow"), None, None),
        P(("wide", "narrow"), None, None),
        P(None, "narrow"),
        P(None, "narrow"),
    )
    return jax.shard_map(
        functools.partial(shards, mesh.shape["wide"], mesh.shape["narrow"]),
        mesh=mesh,
        in_specs=placed,
        out_specs=(P(("wide", "narrow"), None), P("wide", "narrow")),
        check_vma=False,
    )
```
